128 devices in a mesh: dp: 8 (over z, core), ctx: 16 (over x, y).
Axes of the slice: x: 4, y: 4, z: 4, core: 2. Of those that a mesh axis runs over, the one named last changes fastest.
Arguments:
- queries: bfloat16 [32768, 1024], P(('dp', 'ctx')), may hold values from -27 to 27, as said below
- keys: bfloat16 [32768, 128], P(('dp', 'ctx')), may hold values from -4 to 4, as said below
- values: bfloat16 [32768, 128], P(('dp', 'ctx')), may hold values from -6 to 6
- grad_out: bfloat16 [32768, 1024], P(('dp', 'ctx')), may hold values from -6 to 6
- lengths: int32 [32], replicated, may hold values from 1 to 4096, 32768 in all
Outputs:
- attn_out: bfloat16 [32768, 1024], P(('dp', 'ctx'))
- grad_queries: bfloat16 [32768, 1024], P(('dp', 'ctx'))
- grad_keys: bfloat16 [32768, 128], P(('dp', 'ctx'))
- grad_values: bfloat16 [32768, 128], P(('dp', 'ctx'))
The draws below stay inside these ranges and needn't reach their ends.
Inputs may be any that keep to these rules, and one draw needn't show every extreme that they name: `queries`: query entries lie in this range. `keys`: key entries lie in this range.
All inputs are finite; a program needn't handle non-finite values.
Results may differ from the reference program's by a relative error of at most 0.029.
Values may be sent and summed in bfloat16 or wider, within the bound.
A program may use at most 192 MiB of HBM per device.

```python
import math
import jax
import jax.numpy as jnp
import numpy as np
from jax import lax

HEADS = 8
HDIM = 128
T_DEV = 256
WIN = 16
MAXLEN = 4096
TOKENS = 32768
NDOCS = 32


def draw_queries(key, part):
    normal_rows = jax.random.normal(jax.random.fold_in(key, 201), (TOKENS, HEADS * HDIM), jnp.float32)
    return jnp.clip(normal_rows, -6.0, 6.0).astype(jnp.bfloat16)


def draw_keys(key, part):
    normal_rows = jax.random.normal(jax.random.fold_in(key, 202), (TOKENS, HDIM), jnp.float32)
    return jnp.clip(normal_rows, -4.0, 4.0).astype(jnp.bfloat16)


def steps_of(rng, dims, cuts, least, largest):
    factor_of, own = 1.0, jax.random.fold_in(rng, 6)
    for dim, shards_of in cuts:
        steps = jnp.exp(jax.random.uniform(jax.random.fold_in(own, dim), (shards_of,), jnp.float32, least / len(cuts), largest / len(cuts)))
        factor_of = factor_of * jnp.repeat(steps, dims[dim] // shards_of).reshape([-1 if axis == dim else 1 for axis in range(len(dims))])
    return factor_of


def profile(amount, total, limit, lean):
    portions = [(1 << 20) // math.isqrt(grade ** lean) + 1 for grade in range(2, amount + 1)]
    rest, given = total - limit - (amount - 1), [1] * (amount - 1)
    while rest > 0:
        candidates = [i for i in range(amount - 1) if given[i] < limit]
        whole, budget = sum([portions[i] for i in candidates]), rest
        for i in candidates:
            more = min(limit - given[i], max(1, budget * portions[i] // whole), rest)
            given[i] = given[i] + more
            rest = rest - more
    return np.array([limit] + given)


def uneven(stream_key, amount, total, reach, slope):
    if amount == 2:
        one = jax.random.randint(stream_key, (), max(1, total - reach), min(reach, total - 1) + 1)
        return jnp.stack([one, total - one])
    tallies = jnp.asarray(profile(amount, total, reach, slope), jnp.int32)
    couples = (amount - 1) // 2
    donor, taker = tallies[1:1 + 2 * couples:2], tallies[2:2 + 2 * couples:2]
    room = jnp.minimum(donor - 1, reach - taker)
    moved = jax.random.randint(jax.random.fold_in(stream_key, 1), (couples,), 0, 1 << 20) % (room + 1)
    tallies = tallies.at[1:1 + 2 * couples:2].set(donor - moved).at[2:2 + 2 * couples:2].set(taker + moved)
    return tallies[jax.random.permutation(jax.random.fold_in(stream_key, 2), amount)]


def scatter_about(rng, extent, width, limit, shards=(), held_as=jnp.bfloat16):
    result = width * jax.random.normal(rng, extent, jnp.float32)
    if shards:
        result = result * steps_of(rng, extent, shards, -0.22, 0.18)
    return jnp.clip(result, -limit, limit).astype(held_as)


def setup_inputs(seed: int = 0) -> dict:
    arg_keys = jax.random.split(jax.random.key(seed), 6)
    queries = draw_queries(jax.random.fold_in(arg_keys[5], 71), 0)
    keys = draw_keys(jax.random.fold_in(arg_keys[5], 71), 0)
    values = scatter_about(arg_keys[2], (TOKENS, HDIM), 1.0, 6.0, ((0, 128),))
    grad_out = scatter_about(arg_keys[3], (TOKENS, HEADS * HDIM), 1.0, 6.0, ((0, 128),))
    lengths = uneven(arg_keys[4], NDOCS, TOKENS, MAXLEN, 2).astype(jnp.int32)
    return {"queries": queries, "keys": keys, "values": values, "grad_out": grad_out, "lengths": lengths}


NEG_FILL = -1e30


def reference(queries, keys, values, grad_out, lengths):
    rows = T_DEV
    span = (WIN + 1) * rows
    margin = WIN * rows
    scale = float(HDIM) ** -0.5
    ends = jnp.cumsum(lengths).astype(jnp.int32)
    position = jnp.arange(TOKENS, dtype=jnp.int32)
    doc_ids = jnp.sum((ends[None, :] <= position[:, None]).astype(jnp.int32), axis=1).astype(jnp.int32)
    keys_pad = jnp.concatenate([jnp.zeros((margin, HDIM), keys.dtype), keys], axis=0)
    values_pad = jnp.concatenate([jnp.zeros((margin, HDIM), values.dtype), values], axis=0)
    docs_pad = jnp.concatenate([jnp.full((margin,), -1, jnp.int32), doc_ids], axis=0)

    def step(carry, block):
        key_acc, value_acc = carry
        start = (block * rows).astype(jnp.int32)
        query_flat = lax.dynamic_slice_in_dim(queries, start, rows, 0).reshape(rows * HEADS, HDIM)
        grad_flat = lax.dynamic_slice_in_dim(grad_out, start, rows, 0).reshape(rows * HEADS, HDIM)
        key_win = lax.dynamic_slice_in_dim(keys_pad, start, span, 0)
        value_win = lax.dynamic_slice_in_dim(values_pad, start, span, 0)
        query_doc = lax.dynamic_slice_in_dim(doc_ids, start, rows, 0)
        key_doc = lax.dynamic_slice_in_dim(docs_pad, start, span, 0)
        query_pos = start + jnp.arange(rows, dtype=jnp.int32)
        key_pos = start - margin + jnp.arange(span, dtype=jnp.int32)
        allowed = ((query_doc[:, None] == key_doc[None, :]) & (key_pos[None, :] <= query_pos[:, None]))[:, None, :]
        scores = (jnp.dot(query_flat, key_win.T, preferred_element_type=jnp.float32) * scale).reshape(rows, HEADS, span)
        row_max = jnp.max(jnp.where(allowed, scores, NEG_FILL), axis=-1)
        row_total = jnp.sum(jnp.where(allowed, jnp.exp(scores - row_max[..., None]), 0.0), axis=-1)
        logsum = row_max + jnp.log(row_total)
        probs = jnp.where(allowed, jnp.exp(scores - logsum[..., None]), 0.0)
        prob_half = probs.astype(jnp.bfloat16).reshape(rows * HEADS, span)
        output = jnp.dot(prob_half, value_win, preferred_element_type=jnp.float32).astype(jnp.bfloat16)
        correction = jnp.sum(grad_flat.astype(jnp.float32) * output.astype(jnp.float32), axis=1).reshape(rows, HEADS)
        dprob = jnp.dot(grad_flat, value_win.T, preferred_element_type=jnp.float32).reshape(rows, HEADS, span)
        dscore_half = (probs * (dprob - correction[..., None])).astype(jnp.bfloat16).reshape(rows * HEADS, span)
        grad_query = (jnp.dot(dscore_half, key_win, preferred_element_type=jnp.float32) * scale).astype(jnp.bfloat16)
        key_term = jnp.dot(dscore_half.T, query_flat, preferred_element_type=jnp.float32)
        value_term = jnp.dot(prob_half.T, grad_flat, preferred_element_type=jnp.float32)
        key_acc = lax.dynamic_update_slice_in_dim(key_acc, lax.dynamic_slice_in_dim(key_acc, start, span, 0) + key_term, start, 0)
        value_acc = lax.dynamic_update_slice_in_dim(value_acc, lax.dynamic_slice_in_dim(value_acc, start, span, 0) + value_term, start, 0)
        return (key_acc, value_acc), (output.reshape(rows, HEADS * HDIM), grad_query.reshape(rows, HEADS * HDIM))

    blocks = jnp.arange(TOKENS // rows, dtype=jnp.int32)
    start_acc = (jnp.zeros((TOKENS + margin, HDIM), jnp.float32), jnp.zeros((TOKENS + margin, HDIM), jnp.float32))
    (key_acc, value_acc), (outputs, grad_queries) = lax.scan(step, start_acc, blocks)
    attn_out = outputs.reshape(TOKENS, HEADS * HDIM)
    grad_q = grad_queries.reshape(TOKENS, HEADS * HDIM)
    grad_keys = (key_acc[margin:] * scale).astype(jnp.bfloat16)
    grad_values = value_acc[margin:].astype(jnp.bfloat16)
    return (attn_out, grad_q, grad_keys, grad_values)
```

```python
import functools
import math

import jax
import jax.numpy as jnp
from jax import lax
from jax.experimental import pallas as pl
from jax.experimental.pallas import tpu as pltpu
from jax.sharding import PartitionSpec as P

HEADS = 8
HDIM = 128
ROWS = 256
NDOCS = 32
SCALE = float(HDIM) ** -0.5
LOG2_SCALE = SCALE * math.log2(math.e)
BIG = 2.0**20
MESH = pl.DeviceIdType.MESH
F32 = jnp.float32
BF16 = jnp.bfloat16
FWD_UNROLL = 2
COMM = True


def dot(a, b, ca, cb):
    return lax.dot_general(a, b, (((ca,), (cb,)), ((), ())), preferred_element_type=F32)


def kernel(
    len_ref, q_ref, k_ref, v_ref, g_ref, o_ref, dq_ref, dk_ref, dv_ref,
    kb, vb, fk, qa, qt, gh, gs, gt, eb, db, mb, acc, lse, corr,
    pk, pv, rk, rv, rk2, rv2, rk3, rv3, ak, av, sk, sv, sk3, sv3,
    loc, kc, vc, kx, ky, vy, vx, bky, bvx, bkx, bvy, bkc, bvc,
):
    dp, ctx = lax.axis_index("dp"), lax.axis_index("ctx")
    x, y = ctx // 4, lax.rem(ctx, 4)
    block = dp * 16 + ctx
    ahead = (lax.rem(dp + 1, 8), ctx)
    behind = (lax.rem(dp + 7, 8), ctx)

    def along_x(i):
        return (dp, lax.rem(x + i + 4, 4) * 4 + y)

    def along_y(j):
        return (dp, x * 4 + lax.rem(y + j + 4, 4))

    def remote(src, dst, sems, index, device):
        return pltpu.make_async_remote_copy(
            src_ref=src, dst_ref=dst, send_sem=sems.at[(0,) + index], recv_sem=sems.at[(1,) + index],
            device_id=device, device_id_type=MESH,
        )

    own = [
        pltpu.make_async_copy(k_ref, kb.at[4], loc.at[0]),
        pltpu.make_async_copy(v_ref, vb.at[y * 5 + 4], loc.at[1]),
    ]
    for copy in own:
        copy.start()
    if COMM:
        barrier = pltpu.get_barrier_semaphore()
        for device in [along_x(1), along_x(2), along_x(3), along_y(1), along_y(2), along_y(3), ahead, behind]:
            pl.semaphore_signal(barrier, inc=1, device_id=device, device_id_type=MESH)
    for copy in own:
        copy.wait()

    def k_cross():
        return remote(k_ref, kb.at[0], kc, (0,), ahead)

    def v_cross():
        return remote(v_ref, vb.at[y * 5], vc, (0,), ahead)

    def k_x(i):
        wrap = (x + i >= 4).astype(jnp.int32)
        return remote(kb.at[4 - 4 * wrap], kb.at[4 - i], kx, (i - 1,), along_x(i))

    def k_y(j, r):
        wrap = (y + j >= 4).astype(jnp.int32)
        return remote(kb.at[r - wrap], kb.at[4 * j + r], ky, (j - 1, r - 1), along_y(j))

    def v_y(j, old):
        slot = y * 5 + (0 if old else 4)
        return remote(vb.at[slot], vb.at[slot], vy, (j - 1, old), along_y(j))

    def v_x(i, c):
        wrap = (x + i >= 4).astype(jnp.int32)
        return remote(vb.at[c * 5 + 4 - 4 * wrap], vb.at[c * 5 + 4 - i], vx, (i - 1, c), along_x(i))

    if COMM:
        pl.semaphore_wait(barrier, 8)
        k_cross().start()
        v_cross().start()
        for i in (1, 3, 2):
            @pl.when(x + i < 4)
            def _():
                k_x(i).start()
                v_x(i, y).start()
        for j in (1, 3, 2):
            v_y(j, 0).start()
            @pl.when(y + j < 4)
            def _():
                k_y(j, 4).start()

    lane = lax.broadcasted_iota(jnp.int32, (1, HDIM), 1)
    starts = jnp.zeros((1, HDIM), jnp.int32)
    stops = jnp.zeros((1, HDIM), jnp.int32)
    total = jnp.int32(0)
    for d in range(NDOCS):
        starts = jnp.where(lane == d, total, starts)
        total = total + len_ref[d]
        stops = jnp.where(lane == d, total, stops)
    place = lax.broadcasted_iota(jnp.int32, (ROWS, HDIM), 0)

    def member(start):
        position = place + start
        return (position >= starts) & (position < stops)

    query_member = jnp.where(member(block * ROWS), 1.0, 0.0).astype(BF16)
    for h in range(HEADS):
        heads = pl.ds(h * HDIM, HDIM)
        query = q_ref[:, heads]
        qa[h, :, :HDIM] = query
        qa[h, :, HDIM:] = query_member
        qt[:, pl.ds(h * ROWS, ROWS)] = query.T
        gh[h] = g_ref[:, heads]

    @pl.loop(0, 17)
    def _(index):
        group = jnp.maximum(index - 1, 0) // 4
        back = group + 4 * (4 - (index - 4 * group))
        fk[index] = jnp.where(member((block - back) * ROWS), 0.0, -BIG).astype(BF16)

    ones = jnp.ones((ROWS, HDIM), BF16)

    def head_rows(h):
        return pl.ds(pl.multiple_of(h * ROWS, ROWS), ROWS)

    def forward(slot, k0, v0, blocks):
        def body(h, carry):
            scores = [
                dot(qa[h], jnp.concatenate([kb[k0 + n], fk[k0 + n]], axis=1), 1, 1) for n in range(blocks)
            ]
            if slot is None:
                row = lax.broadcasted_iota(jnp.int32, (ROWS, ROWS), 0)
                column = lax.broadcasted_iota(jnp.int32, (ROWS, ROWS), 1)
                scores = [jnp.where(column <= row, scores[0], -BIG)]
            top = functools.reduce(jnp.maximum, [s[:, half] for s in scores for half in (slice(0, 128), slice(128, 256))])
            top = jnp.max(top, axis=1, keepdims=True)
            here = 0 if slot is None else slot
            if slot is None:
                peak = jnp.broadcast_to(top, (ROWS, HDIM))
            else:
                before = mb[here - 1, h]
                peak = jnp.maximum(before, top)
            mb[here, h] = peak
            peak2 = jnp.concatenate([peak, peak], axis=1) * LOG2_SCALE
            term = None
            for n in range(blocks):
                weights = jnp.exp2(scores[n] * LOG2_SCALE - peak2).astype(BF16)
                eb[k0 + n, head_rows(h), :] = weights
                part = dot(weights, jnp.concatenate([vb[v0 + n], ones], axis=1), 1, 0)
                term = part if term is None else term + part
            if slot is None:
                acc[h] = term
            else:
                shrink = jnp.exp2((before - peak) * LOG2_SCALE)
                acc[h] = acc[h] * jnp.concatenate([shrink, shrink], axis=1) + term
            return carry

        lax.fori_loop(0, HEADS, body, 0, unroll=FWD_UNROLL)

    forward(None, 4, y * 5 + 4, 1)

    if COMM:
        k_cross().wait_recv()
        v_cross().wait_recv()
        for i in (1, 3, 2):
            @pl.when(x + i >= 4)
            def _():
                k_x(i).start()
                v_x(i, y).start()
        for j in (1, 3, 2):
            v_y(j, 1).start()
        for i in (3, 1, 2):
            k_x(i).wait_recv()
        for r in (4, 3, 2, 1):
            for j in (1, 3, 2):
                if r == 4:
                    @pl.when(y + j >= 4)
                    def _():
                        k_y(j, 4).start()
                else:
                    k_y(j, r).start()
        for j in (1, 3, 2):
            for old in (0, 1):
                v_y(j, old).wait_recv()
        for j in (1, 3, 2):
            column = lax.rem(y - j + 4, 4)
            for i in (1, 3, 2):
                v_x(i, column).start()

    @pl.loop(0, 4)
    def _(j):
        column = lax.rem(y - j + 4, 4)
        wrap = (j > y).astype(jnp.int32)
        first = jnp.minimum(j, 1)
        if COMM:
            for i in (1, 2, 3):
                v_x(i, column).wait_recv()

            @pl.when(j > 0)
            def _():
                for r in (1, 2, 3, 4):
                    k_y(j, r).wait_recv()
        forward(j + 1, 4 * j + first, column * 5 + first - wrap, 4)

    for h in range(HEADS):
        heads = pl.ds(h * HDIM, HDIM)
        norm = acc[h, :, HDIM:]
        result = (acc[h, :, :HDIM] / norm).astype(BF16)
        o_ref[:, heads] = result
        lse[h] = mb[4, h] * LOG2_SCALE + jnp.log2(norm)
        total = jnp.sum(gh[h].astype(F32) * result.astype(F32), axis=1, keepdims=True)
        corr[h] = jnp.broadcast_to(total, (ROWS, HDIM))

    av[...] = jnp.zeros_like(av)

    def gk_y(j, r):
        return remote(pk.at[4 * j + r], rk.at[j - 1, r - 1], bky, (j - 1, r - 1), along_y(-j))

    def gv_x(i, c):
        return remote(pv.at[c * 5 + 4 - i], rv.at[i - 1, c], bvx, (i - 1, c), along_x(-i))

    def scale_group(slot):
        for h in range(HEADS):
            factor = jnp.exp2(mb[slot, h] * LOG2_SCALE - lse[h])
            scaled = (gh[h].astype(F32) * factor).astype(BF16)
            gs[h] = scaled
            gt[:, pl.ds(h * ROWS, ROWS)] = scaled.T
            acc[h, :, :HDIM] = corr[h] * factor

    def backward(k, v):
        for h in range(HEADS):
            rows = pl.ds(h * ROWS, ROWS)
            dprob = dot(gs[h], vb[v], 1, 1)
            shift = acc[h, :, :HDIM]
            shift = jnp.concatenate([shift, shift], axis=1)
            db[k, rows, :] = (eb[k, rows, :].astype(F32) * (dprob - shift)).astype(BF16)
        value_term = dot(gt[...], eb[k], 1, 0)
        key_term = dot(qt[...], db[k], 1, 0)
        return key_term, value_term

    @pl.loop(1, 5)
    def _(step):
        j = lax.rem(step, 4)
        column = lax.rem(y - j + 4, 4)
        wrap = (j > y).astype(jnp.int32)
        first = jnp.minimum(j, 1)
        scale_group(j + 1)

        @pl.loop(0, 4)
        def _(n):
            r = first + n
            row = r - wrap
            key_term, value_term = backward(4 * j + r, column * 5 + row)

            @pl.when(j > 0)
            def _():
                pk[4 * j + r] = key_term.astype(BF16)
                if COMM:
                    gk_y(j, r).start()

            @pl.when(j == 0)
            def _():
                ak[r] = key_term

            @pl.when((row > 0) & (row < 4))
            def _():
                pv[column * 5 + row] = value_term.astype(BF16)
                if COMM:
                    gv_x(4 - row, column).start()

            @pl.when((row == 0) | (row == 4))
            def _():
                av[row // 4, column] = value_term

    scale_group(0)
    key_term, value_term = backward(4, y * 5 + 4)
    ak[4] = key_term
    av[1, y] = value_term

    def gk_x(i):
        return remote(sk.at[i - 1], rk2.at[i - 1], bkx, (i - 1,), along_x(-i))

    def gv_y(j, old):
        return remote(sv.at[j - 1, old], rv2.at[j - 1, old], bvy, (j - 1, old), along_y(-j))

    def gk_cross():
        return remote(sk3, rk3, bkc, (0,), behind)

    def gv_cross():
        return remote(sv3, rv3, bvc, (0,), behind)

    if COMM:
        for j in (1, 2, 3):
            for r in (1, 2, 3, 4):
                gk_y(j, r).wait_recv()
        for h in (1, 2, 3, 0, 4):
            total = ak[h]
            for j in (1, 2, 3):
                wrap = (y + j >= 4).astype(jnp.int32)
                if h in (1, 2, 3):
                    total = total + rk[j - 1, h + wrap - 1].astype(F32)
                else:
                    hit = (wrap == 1) if h == 0 else (wrap == 0)
                    total = total + jnp.where(hit, rk[j - 1, 0 if h == 0 else 3].astype(F32), 0.0)
            if h in (1, 2, 3):
                sk[4 - h - 1] = total.astype(BF16)
                gk_x(4 - h).start()
            else:
                ak[h] = total
        for i in (1, 2, 3):
            for c in range(4):
                gv_x(i, c).wait_recv()
        for j in (1, 2, 3, 0):
            column = lax.rem(y - j + 4, 4)
            for old in (0, 1):
                total = av[1 - old, column]
                for i in (1, 2, 3):
                    hit = (x + i >= 4) if old else (x + i < 4)
                    total = total + jnp.where(hit, rv[i - 1, column].astype(F32), 0.0)
                if j > 0:
                    sv[j - 1, old] = total.astype(BF16)
                    gv_y(j, old).start()
                else:
                    av[1 - old, column] = total

    for h in range(HEADS):
        total = None
        for k in range(17):
            part = dot(db[k, pl.ds(h * ROWS, ROWS), :], kb[k], 1, 0)
            total = part if total is None else total + part
        dq_ref[:, pl.ds(h * HDIM, HDIM)] = (total * SCALE).astype(BF16)

    key_total, value_total = ak[4], av[1, y]
    if COMM:
        key_old = ak[0]
        for i in (1, 2, 3):
            gk_x(i).wait_recv()
            arrived = rk2[i - 1].astype(F32)
            key_old = key_old + jnp.where(x + i >= 4, arrived, 0.0)
            key_total = key_total + jnp.where(x + i < 4, arrived, 0.0)
        sk3[...] = key_old.astype(BF16)
        gk_cross().start()
        value_old = av[0, y]
        for j in (1, 2, 3):
            gv_y(j, 1).wait_recv()
            value_old = value_old + rv2[j - 1, 1].astype(F32)
        sv3[...] = value_old.astype(BF16)
        gv_cross().start()
        for j in (1, 2, 3):
            gv_y(j, 0).wait_recv()
            value_total = value_total + rv2[j - 1, 0].astype(F32)
        gk_cross().wait_recv()
        key_total = key_total + rk3[...].astype(F32)
        gv_cross().wait_recv()
        value_total = value_total + rv3[...].astype(F32)
    dk_ref[...] = (key_total * SCALE).T.astype(BF16)
    dv_ref[...] = value_total.T.astype(BF16)

    if COMM:
        k_cross().wait_send()
        v_cross().wait_send()
        for i in (1, 2, 3):
            k_x(i).wait_send()
            for c in range(4):
                v_x(i, c).wait_send()
                gv_x(i, c).wait_send()
            gk_x(i).wait_send()
        for j in (1, 2, 3):
            for r in (1, 2, 3, 4):
                k_y(j, r).wait_send()
                gk_y(j, r).wait_send()
            for old in (0, 1):
                v_y(j, old).wait_send()
                gv_y(j, old).wait_send()
        gk_cross().wait_send()
        gv_cross().wait_send()


def shards(queries, keys, values, grad_out, lengths):
    vmem = pl.BlockSpec(memory_space=pltpu.VMEM)
    block = (ROWS, HDIM)
    turned = (HDIM, ROWS)
    dma = pltpu.SemaphoreType.DMA
    return pl.pallas_call(
        kernel,
        out_shape=(
            jax.ShapeDtypeStruct((ROWS, HEADS * HDIM), BF16),
            jax.ShapeDtypeStruct((ROWS, HEADS * HDIM), BF16),
            jax.ShapeDtypeStruct(block, BF16),
            jax.ShapeDtypeStruct(block, BF16),
        ),
        in_specs=[pl.BlockSpec(memory_space=pltpu.SMEM), vmem, vmem, vmem, vmem],
        out_specs=(vmem, vmem, vmem, vmem),
        scratch_shapes=[
            pltpu.VMEM((17,) + block, BF16),
            pltpu.VMEM((20,) + block, BF16),
            pltpu.VMEM((17,) + block, BF16),
            pltpu.VMEM((HEADS, ROWS, 2 * HDIM), BF16),
            pltpu.VMEM((HDIM, HEADS * ROWS), BF16),
            pltpu.VMEM((HEADS,) + block, BF16),
            pltpu.VMEM((HEADS,) + block, BF16),
            pltpu.VMEM((HDIM, HEADS * ROWS), BF16),
            pltpu.VMEM((17, HEADS * ROWS, ROWS), BF16),
            pltpu.VMEM((17, HEADS * ROWS, ROWS), BF16),
            pltpu.VMEM((5, HEADS) + block, F32),
            pltpu.VMEM((HEADS, ROWS, 2 * HDIM), F32),
            pltpu.VMEM((HEADS,) + block, F32),
            pltpu.VMEM((HEADS,) + block, F32),
            pltpu.VMEM((17,) + turned, BF16),
            pltpu.VMEM((20,) + turned, BF16),
            pltpu.VMEM((3, 4) + turned, BF16),
            pltpu.VMEM((3, 4) + turned, BF16),
            pltpu.VMEM((3,) + turned, BF16),
            pltpu.VMEM((3, 2) + turned, BF16),
            pltpu.VMEM(turned, BF16),
            pltpu.VMEM(turned, BF16),
            pltpu.VMEM((5,) + turned, F32),
            pltpu.VMEM((2, 4) + turned, F32),
            pltpu.VMEM((3,) + turned, BF16),
            pltpu.VMEM((3, 2) + turned, BF16),
            pltpu.VMEM(turned, BF16),
            pltpu.VMEM(turned, BF16),
            dma((2,)),
            dma((2, 1)),
            dma((2, 1)),
            dma((2, 3)),
            dma((2, 3, 4)),
            dma((2, 3, 2)),
            dma((2, 3, 4)),
            dma((2, 3, 4)),
            dma((2, 3, 4)),
            dma((2, 3)),
            dma((2, 3, 2)),
            dma((2, 1)),
            dma((2, 1)),
        ],
        compiler_params=pltpu.CompilerParams(
            collective_id=0 if COMM else None, has_side_effects=COMM, vmem_limit_bytes=67043328
        ),
        name="attention",
    )(lengths, queries, keys, values, grad_out)


def solution(mesh):
    spread = P(("dp", "ctx"), None)
    return jax.shard_map(
        shards,
        mesh=mesh,
        in_specs=(spread, spread, spread, spread, P()),
        out_specs=(spread, spread, spread, spread),
        check_vma=False,
    )
```

```python
import functools
import math

import jax
import jax.numpy as jnp
from jax import lax
from jax.experimental import pallas as pl
from jax.experimental.pallas import tpu as pltpu
from jax.sharding import PartitionSpec as P

HEADS = 8
HDIM = 128
ROWS = 256
NDOCS = 32
SCALE = float(HDIM) ** -0.5
LOG2_SCALE = SCALE * math.log2(math.e)
BIG = 2.0**20
MESH = pl.DeviceIdType.MESH
F32 = jnp.float32
BF16 = jnp.bfloat16
FWD_UNROLL = 8
OUT_UNROLL = 8
VALUES_AT = 11
COMM = True


def dot(a, b, ca, cb):
    return lax.dot_general(a, b, (((ca,), (cb,)), ((), ())), preferred_element_type=F32)


def kernel(
    len_ref, q_ref, k_ref, v_ref, g_ref, o_ref, dq_ref, dk_ref, dv_ref,
    kb, vb, fk, qa, qt, gh, gs, gt, eb, mb, acc, tot,
    pk, pv, rk, rv, rk2, rv2, ak, av, sk, sv,
    loc, kx, ky, vy, vx, bky, bvx, bkx, bvy,
):
    dp, ctx = lax.axis_index("dp"), lax.axis_index("ctx")
    x, y = ctx // 4, lax.rem(ctx, 4)
    block = dp * 16 + ctx

    def along_x(i, plane=0):
        return (lax.rem(dp + plane + 8, 8), lax.rem(x + i + 4, 4) * 4 + y)

    def along_y(j, plane=0):
        return (lax.rem(dp + plane + 8, 8), x * 4 + lax.rem(y + j + 4, 4))

    def remote(src, dst, sems, index, device):
        return pltpu.make_async_remote_copy(
            src_ref=src, dst_ref=dst, send_sem=sems.at[(0,) + index], recv_sem=sems.at[(1,) + index],
            device_id=device, device_id_type=MESH,
        )

    own = [
        pltpu.make_async_copy(k_ref, kb.at[4], loc.at[0]),
        pltpu.make_async_copy(v_ref, vb.at[y * 5 + 4], loc.at[1]),
    ]
    for copy in own:
        copy.start()
    if COMM:
        barrier = pltpu.get_barrier_semaphore()

        def greet(device):
            pl.semaphore_signal(barrier, inc=1, device_id=device, device_id_type=MESH)

        for i in (1, 2, 3):
            greet(along_x(i))
            greet(along_y(i))
            greet(along_x(i, jnp.where(x + i >= 4, 1, -1)))
            greet(along_y(i, 1))
            greet(along_y(i, -1))
        greet(along_y(0, 1))
        greet(along_y(0, -1))
    for copy in own:
        copy.wait()

    def wraps(at, steps):
        return (at + steps >= 4).astype(jnp.int32)

    def k_x(i):
        return remote(k_ref, kb.at[4 - i], kx, (i - 1,), along_x(i, wraps(x, i)))

    def k_y(j, r):
        return remote(kb.at[r - wraps(y, j)], kb.at[4 * j + r], ky, (j - 1, r - 1), along_y(j))

    def v_y(j, old):
        return remote(v_ref, vb.at[y * 5 + (0 if old else 4)], vy, (j, old), along_y(j, old))

    def v_own(i):
        return remote(v_ref, vb.at[y * 5 + 4 - i], vx, (i - 1, y), along_x(i, wraps(x, i)))

    def v_x(i, c):
        return remote(vb.at[c * 5 + 4 - 4 * wraps(x, i)], vb.at[c * 5 + 4 - i], vx, (i - 1, c), along_x(i))

    v_first = [(j, old) for old in (0, 1) for j in (1, 3, 2)] + [(0, 1)]
    if COMM:
        pl.semaphore_wait(barrier, 17)
        for i in (1, 3, 2, 4):
            k_x(i).start()
        for j, old in v_first:
            v_y(j, old).start()
        for j in (1, 3, 2):
            @pl.when(y + j < 4)
            def _():
                k_y(j, 4).start()
        for i in (1, 3, 2):
            v_own(i).start()

    lane = lax.broadcasted_iota(jnp.int32, (1, HDIM), 1)
    starts = jnp.zeros((1, HDIM), jnp.int32)
    stops = jnp.zeros((1, HDIM), jnp.int32)
    total = jnp.int32(0)
    for d in range(NDOCS):
        starts = jnp.where(lane == d, total, starts)
        total = total + len_ref[d]
        stops = jnp.where(lane == d, total, stops)
    place = lax.broadcasted_iota(jnp.int32, (ROWS, HDIM), 0)

    def member(start):
        position = place + start
        return (position >= starts) & (position < stops)

    query_member = jnp.where(member(block * ROWS), 1.0, 0.0).astype(BF16)
    for h in range(HEADS):
        heads = pl.ds(h * HDIM, HDIM)
        qa[h, :, :HDIM] = q_ref[:, heads]
        qa[h, :, HDIM:] = query_member
        gh[h] = g_ref[:, heads]

    @pl.loop(0, 17)
    def _(index):
        group = jnp.maximum(index - 1, 0) // 4
        back = group + 4 * (4 - (index - 4 * group))
        fk[index] = jnp.where(member((block - back) * ROWS), 0.0, -BIG).astype(BF16)

    def head_rows(h):
        return pl.ds(pl.multiple_of(h * ROWS, ROWS), ROWS)

    def halves(tiles):
        return [t[:, half] for t in tiles for half in (slice(0, HDIM), slice(HDIM, 2 * HDIM))]

    def forward(slot, k0, v0, blocks, ready=None):
        def body(h, carry):
            scores = [
                dot(qa[h], jnp.concatenate([kb[k0 + n], fk[k0 + n]], axis=1), 1, 1) for n in range(blocks)
            ]
            if slot is None:
                row = lax.broadcasted_iota(jnp.int32, (ROWS, ROWS), 0)
                column = lax.broadcasted_iota(jnp.int32, (ROWS, ROWS), 1)
                scores = [jnp.where(column <= row, scores[0], -BIG)]
            top = functools.reduce(jnp.maximum, halves(scores))
            top = jnp.max(top, axis=1, keepdims=True)
            if slot is None:
                peak = jnp.broadcast_to(top, (ROWS, HDIM))
                mb[0, h] = peak
            else:
                before = mb[slot - 1, h]
                peak = jnp.maximum(before, top)
                mb[slot, h] = peak
            peak2 = jnp.concatenate([peak, peak], axis=1) * LOG2_SCALE
            weights = [jnp.exp2(score * LOG2_SCALE - peak2) for score in scores]
            part = functools.reduce(jnp.add, halves(weights))
            for n in range(blocks):
                eb[k0 + n, head_rows(h), :] = weights[n].astype(BF16)
            if slot is None:
                tot[h] = part
            else:
                tot[h] = tot[h] * jnp.exp2((before - peak) * LOG2_SCALE) + part
            return carry

        def gather(h, carry):
            weights = jnp.concatenate([eb[k0 + n, head_rows(h), :] for n in range(blocks)], axis=1)
            term = dot(weights, vb[pl.ds(v0, blocks)].reshape(blocks * ROWS, HDIM), 1, 0)
            if slot is None:
                acc[h] = term
            else:
                acc[h] = acc[h] * jnp.exp2((mb[slot - 1, h] - mb[slot, h]) * LOG2_SCALE) + term
            return carry

        lax.fori_loop(0, HEADS, body, 0, unroll=FWD_UNROLL)
        if ready is not None:
            ready()
        lax.fori_loop(0, HEADS, gather, 0, unroll=OUT_UNROLL)

    forward(None, 4, y * 5 + 4, 1)

    if COMM:
        for i in (1, 3, 2, 4):
            k_x(i).wait_recv()
        for j in (1, 3, 2):
            @pl.when(y + j >= 4)
            def _():
                k_y(j, 4).start()
            for r in (3, 2, 1):
                k_y(j, r).start()
        for j, old in v_first:
            v_y(j, old).wait_recv()
        for j in (1, 3, 2):
            for i in (1, 3, 2):
                v_x(i, lax.rem(y - j + 4, 4)).start()
        for i in (1, 3, 2):
            v_own(i).wait_recv()

    forward(1, 0, y * 5, 4)

    for h in range(HEADS):
        qt[:, pl.ds(h * ROWS, ROWS)] = q_ref[:, pl.ds(h * HDIM, HDIM)].T

    @pl.loop(0, 3)
    def _(step):
        j = 1 + lax.rem(2 * step, 3)
        column = lax.rem(y - j + 4, 4)
        wrap = (j > y).astype(jnp.int32)
        if COMM:
            for r in (1, 2, 3, 4):
                k_y(j, r).wait_recv()

        def ready():
            for i in (1, 2, 3):
                v_x(i, column).wait_recv()

        forward(step + 2, 4 * j + 1, column * 5 + 1 - wrap, 4, ready if COMM else None)

    for h in range(HEADS):
        heads = pl.ds(h * HDIM, HDIM)
        norm = jnp.broadcast_to(jnp.sum(tot[h], axis=1, keepdims=True), (ROWS, HDIM))
        result = (acc[h] / norm).astype(BF16)
        o_ref[:, heads] = result
        grad = gh[h].astype(F32)
        fix = jnp.sum(grad * result.astype(F32), axis=1, keepdims=True)
        top = mb[4, h] * LOG2_SCALE + jnp.log2(norm)
        for slot in range(5):
            factor = jnp.exp2(mb[slot, h] * LOG2_SCALE - top)
            mb[slot, h] = factor * fix
            scaled = (grad * factor).astype(BF16)
            gs[slot, h] = scaled
            gt[slot, :, pl.ds(h * ROWS, ROWS)] = scaled.T

    def slot_of(j):
        return jnp.where(j == 0, 1, 2 + lax.rem(2 * (j - 1), 3))

    def gk_y(j, r):
        return remote(pk.at[4 * j + r], rk.at[j - 1, r - 1], bky, (j - 1, r - 1), along_y(-j))

    def gv_x(i, c):
        return remote(pv.at[c * 5 + 4 - i], rv.at[i - 1, c], bvx, (i - 1, c), along_x(-i))

    def gk_x(i):
        back = (x < i).astype(jnp.int32)
        return remote(sk.at[i - 1], rk2.at[i - 1], bkx, (i - 1,), along_x(-i, -back))

    def gv_y(j, old):
        return remote(sv.at[j, old], rv2.at[j, old], bvy, (j, old), along_y(-j, -old))

    @pl.loop(0, 12)
    def _(n):
        column = n // 3
        row = 1 + lax.rem(lax.rem(n, 3) + 1, 3)
        j = lax.rem(y - column + 4, 4)
        wrap = (j > y).astype(jnp.int32)
        term = dot(gt[slot_of(j)], eb[4 * j + row + wrap], 1, 0)
        pv[column * 5 + row] = term.astype(BF16)
        if COMM:
            gv_x(4 - row, column).start()

    av[...] = jnp.zeros_like(av)
    av[1, y] = dot(gt[0], eb[4], 1, 0)

    @pl.loop(0, 4)
    def _(j):
        column = lax.rem(y - j + 4, 4)
        wrap = (j > y).astype(jnp.int32)
        late = jnp.where((j > 0) & (wrap == 0), 1, 0)
        av[late, column] = dot(gt[slot_of(j)], eb[4 * j + 4 * late + wrap], 1, 0)

    def values_second():
        for i in (1, 3, 2):
            for c in range(4):
                gv_x(i, c).wait_recv()
        for j in (2, 1, 3, 0):
            column = lax.rem(y - j + 4, 4)
            for old in (1, 0):
                total = av[1 - old, column]
                for i in (1, 2, 3):
                    hit = (x + i >= 4) if old else (x + i < 4)
                    total = total + jnp.where(hit, rv[i - 1, column].astype(F32), 0.0)
                if j > 0 or old:
                    sv[j, old] = total.astype(BF16)
                    gv_y(j, old).start()
                else:
                    av[1, column] = total

    def backward(k, v, slot):
        for h in range(HEADS):
            rows = pl.ds(h * ROWS, ROWS)
            dprob = dot(gs[slot, h], vb[v], 1, 1)
            shift = mb[slot, h]
            shift = jnp.concatenate([shift, shift], axis=1)
            eb[k, rows, :] = (eb[k, rows, :].astype(F32) * (dprob - shift)).astype(BF16)
        return dot(qt[...], eb[k], 1, 0)

    def pass_keys(n):
        r = 1 + n // 3
        j = 1 + lax.rem(lax.rem(n, 3) + 1, 3)
        column = lax.rem(y - j + 4, 4)
        wrap = (j > y).astype(jnp.int32)
        pk[4 * j + r] = backward(4 * j + r, column * 5 + r - wrap, slot_of(j)).astype(BF16)
        if COMM:
            gk_y(j, r).start()

    @pl.loop(0, 12)
    def _(n):
        pass_keys(n)
        if COMM:
            @pl.when(n == VALUES_AT)
            def _():
                values_second()

    @pl.loop(0, 5)
    def _(r):
        ak[r] = backward(r, y * 5 + r, jnp.where(r == 4, 0, 1))

    if COMM:
        for j in (1, 2, 3):
            for r in (1, 2, 3, 4):
                gk_y(j, r).wait_recv()
        for h in (0, 2, 1, 3, 4):
            total = ak[h]
            for j in (1, 2, 3):
                wrap = (y + j >= 4).astype(jnp.int32)
                if h in (1, 2, 3):
                    total = total + rk[j - 1, h + wrap - 1].astype(F32)
                else:
                    hit = (wrap == 1) if h == 0 else (wrap == 0)
                    total = total + jnp.where(hit, rk[j - 1, 0 if h == 0 else 3].astype(F32), 0.0)
            if h < 4:
                sk[4 - h - 1] = total.astype(BF16)
                gk_x(4 - h).start()
            else:
                ak[h] = total

    def query_grad(h, carry):
        total = None
        for k in range(17):
            part = dot(eb[k, head_rows(h), :], kb[k], 1, 0)
            total = part if total is None else total + part
        dq_ref[:, pl.ds(pl.multiple_of(h * HDIM, HDIM), HDIM)] = (total * SCALE).astype(BF16)
        return carry

    lax.fori_loop(0, 4, query_grad, 0)

    value_total = av[1, y]
    if COMM:
        for j, old in v_first:
            gv_y(j, old).wait_recv()
            value_total = value_total + rv2[j, old].astype(F32)
    dv_ref[...] = value_total.T.astype(BF16)

    lax.fori_loop(4, HEADS, query_grad, 0)

    key_total = ak[4]
    if COMM:
        for i in (1, 2, 3, 4):
            gk_x(i).wait_recv()
            key_total = key_total + rk2[i - 1].astype(F32)
    dk_ref[...] = (key_total * SCALE).T.astype(BF16)

    if COMM:
        for i in (1, 2, 3, 4):
            k_x(i).wait_send()
            gk_x(i).wait_send()
        for i in (1, 2, 3):
            v_own(i).wait_send()
            for j in (1, 2, 3):
                v_x(i, lax.rem(y - j + 4, 4)).wait_send()
            for c in range(4):
                gv_x(i, c).wait_send()
        for j in (1, 2, 3):
            for r in (1, 2, 3, 4):
                k_y(j, r).wait_send()
                gk_y(j, r).wait_send()
        for j, old in v_first:
            v_y(j, old).wait_send()
            gv_y(j, old).wait_send()


CHUNKS = [(n, c) for n in (0, 1) for c in range(4)] + [(2, 0), (3, 0)]


def deliver(*refs):
    given, taken, held, sems = refs[:4], refs[4:8], refs[8:12], refs[12]

    def piece(n, c):
        return pl.ds(c * (ROWS // 4), ROWS // 4) if n < 2 else pl.ds(0, ROWS)

    def fetch(at, n, c):
        return pltpu.make_async_copy(given[n].at[piece(n, c)], held[n].at[piece(n, c)], sems.at[0, at])

    def store(at, n, c):
        return pltpu.make_async_copy(held[n].at[piece(n, c)], taken[n].at[piece(n, c)], sems.at[1, at])

    for at, chunk in enumerate(CHUNKS):
        fetch(at, *chunk).start()
    for at, chunk in enumerate(CHUNKS):
        fetch(at, *chunk).wait()
        store(at, *chunk).start()
    for at, chunk in enumerate(CHUNKS):
        store(at, *chunk).wait()


def shards(queries, keys, values, grad_out, lengths):
    vmem = pl.BlockSpec(memory_space=pltpu.VMEM)
    block = (ROWS, HDIM)
    turned = (HDIM, ROWS)
    dma = pltpu.SemaphoreType.DMA
    shapes = (
        jax.ShapeDtypeStruct((ROWS, HEADS * HDIM), BF16),
        jax.ShapeDtypeStruct((ROWS, HEADS * HDIM), BF16),
        jax.ShapeDtypeStruct(block, BF16),
        jax.ShapeDtypeStruct(block, BF16),
    )
    results = pl.pallas_call(
        kernel,
        out_shape=shapes,
        in_specs=[pl.BlockSpec(memory_space=pltpu.SMEM), vmem, vmem, vmem, vmem],
        out_specs=(vmem, vmem, vmem, vmem),
        scratch_shapes=[
            pltpu.VMEM((17,) + block, BF16),
            pltpu.VMEM((20,) + block, BF16),
            pltpu.VMEM((17,) + block, BF16),
            pltpu.VMEM((HEADS, ROWS, 2 * HDIM), BF16),
            pltpu.VMEM((HDIM, HEADS * ROWS), BF16),
            pltpu.VMEM((HEADS,) + block, BF16),
            pltpu.VMEM((5, HEADS) + block, BF16),
            pltpu.VMEM((5, HDIM, HEADS * ROWS), BF16),
            pltpu.VMEM((17, HEADS * ROWS, ROWS), BF16),
            pltpu.VMEM((5, HEADS) + block, F32),
            pltpu.VMEM((HEADS,) + block, F32),
            pltpu.VMEM((HEADS,) + block, F32),
            pltpu.VMEM((17,) + turned, BF16),
            pltpu.VMEM((20,) + turned, BF16),
            pltpu.VMEM((3, 4) + turned, BF16),
            pltpu.VMEM((3, 4) + turned, BF16),
            pltpu.VMEM((4,) + turned, BF16),
            pltpu.VMEM((4, 2) + turned, BF16),
            pltpu.VMEM((5,) + turned, F32),
            pltpu.VMEM((2, 4) + turned, F32),
            pltpu.VMEM((4,) + turned, BF16),
            pltpu.VMEM((4, 2) + turned, BF16),
            dma((2,)),
            dma((2, 4)),
            dma((2, 3, 4)),
            dma((2, 4, 2)),
            dma((2, 3, 4)),
            dma((2, 3, 4)),
            dma((2, 3, 4)),
            dma((2, 4)),
            dma((2, 4, 2)),
        ],
        compiler_params=pltpu.CompilerParams(
            collective_id=0 if COMM else None, has_side_effects=COMM, vmem_limit_bytes=67043328
        ),
        name="attention",
    )(lengths, queries, keys, values, grad_out)
    away = pl.BlockSpec(memory_space=pl.ANY)
    return pl.pallas_call(
        deliver,
        out_shape=shapes,
        in_specs=[away] * 4,
        out_specs=(away,) * 4,
        scratch_shapes=[pltpu.VMEM(shape.shape, BF16) for shape in shapes] + [dma((2, len(CHUNKS)))],
        name="deliver",
    )(*results)


def solution(mesh):
    spread = P(("dp", "ctx"), None)
    return jax.shard_map(
        shards,
        mesh=mesh,
        in_specs=(spread, spread, spread, spread, P()),
        out_specs=(spread, spread, spread, spread),
        check_vma=False,
    )
```

```python
import functools
import math

import jax
import jax.numpy as jnp
from jax import lax
from jax.experimental import pallas as pl
from jax.experimental.pallas import tpu as pltpu
from jax.sharding import PartitionSpec as P

HEADS = 8
HDIM = 128
ROWS = 256
NDOCS = 32
SCALE = float(HDIM) ** -0.5
LOG2_SCALE = SCALE * math.log2(math.e)
BIG = 2.0**20
MESH = pl.DeviceIdType.MESH
F32 = jnp.float32
BF16 = jnp.bfloat16
FWD_UNROLL = 8
OUT_UNROLL = 8
VALUES_AT = 11
TAIL_AT = 2
COMM = True


def dot(a, b, ca, cb):
    return lax.dot_general(a, b, (((ca,), (cb,)), ((), ())), preferred_element_type=F32)


def kernel(
    len_ref, q_ref, k_ref, v_ref, g_ref, o_ref, dq_ref, dk_ref, dv_ref,
    kb, vb, fk, qa, qt, gh, gs, gt, eb, mb, tot,
    pk, pv, rk, rv, rk2, rv2, ak, av, sk, sv,
    loc, kx, ky, vy, vx, bky, bvx, bkx, bvy,
):
    dp, ctx = lax.axis_index("dp"), lax.axis_index("ctx")
    x, y = ctx // 4, lax.rem(ctx, 4)
    block = dp * 16 + ctx

    def along_x(i, plane=0):
        return (lax.rem(dp + plane + 8, 8), lax.rem(x + i + 4, 4) * 4 + y)

    def along_y(j, plane=0):
        return (lax.rem(dp + plane + 8, 8), x * 4 + lax.rem(y + j + 4, 4))

    def remote(src, dst, sems, index, device):
        return pltpu.make_async_remote_copy(
            src_ref=src, dst_ref=dst, send_sem=sems.at[(0,) + index], recv_sem=sems.at[(1,) + index],
            device_id=device, device_id_type=MESH,
        )

    own = [
        pltpu.make_async_copy(k_ref, kb.at[y * 5 + 4], loc.at[0]),
        pltpu.make_async_copy(v_ref, vb.at[4], loc.at[1]),
    ]
    for copy in own:
        copy.start()
    if COMM:
        barrier = pltpu.get_barrier_semaphore()

        def greet(device):
            pl.semaphore_signal(barrier, inc=1, device_id=device, device_id_type=MESH)

        for i in (1, 2, 3):
            greet(along_x(i))
            greet(along_y(i))
            greet(along_x(i, jnp.where(x + i >= 4, 1, -1)))
        greet(along_y(0, 1))
        greet(along_y(0, -1))
    for copy in own:
        copy.wait()

    def wraps(at, steps):
        return (at + steps >= 4).astype(jnp.int32)

    def v_x(i):
        return remote(v_ref, vb.at[4 - i], vx, (i - 1,), along_x(i, wraps(x, i)))

    def v_y(j, r):
        return remote(vb.at[r - wraps(y, j)], vb.at[4 * j + r], vy, (j - 1, r - 1), along_y(j))

    def k_y(j):
        return remote(k_ref, kb.at[y * 5 + 4], ky, (j - 1,), along_y(j))

    def k_x(i, c):
        return remote(kb.at[c * 5 + 4], kb.at[c * 5 + 4 - i], kx, (i - 1, c), along_x(i, wraps(x, i)))

    if COMM:
        pl.semaphore_wait(barrier, 11)
        for j in (1, 3, 2):
            k_y(j).start()
        for i in (1, 3, 2, 4):
            k_x(i, y).start()
        for i in (1, 3, 2, 4):
            v_x(i).start()
        for j in (1, 3, 2):
            @pl.when(y + j < 4)
            def _():
                v_y(j, 4).start()

    lane = lax.broadcasted_iota(jnp.int32, (1, HDIM), 1)
    starts = jnp.zeros((1, HDIM), jnp.int32)
    stops = jnp.zeros((1, HDIM), jnp.int32)
    total = jnp.int32(0)
    for d in range(NDOCS):
        starts = jnp.where(lane == d, total, starts)
        total = total + len_ref[d]
        stops = jnp.where(lane == d, total, stops)
    place = lax.broadcasted_iota(jnp.int32, (ROWS, HDIM), 0)

    def member(start):
        position = place + start
        return (position >= starts) & (position < stops)

    query_member = jnp.where(member(block * ROWS), 1.0, 0.0).astype(BF16)
    for h in range(HEADS):
        heads = pl.ds(h * HDIM, HDIM)
        qa[h, :, :HDIM] = q_ref[:, heads]
        qa[h, :, HDIM:] = query_member
        gh[h] = g_ref[:, heads]

    @pl.loop(0, 17)
    def _(index):
        group = jnp.maximum(index - 1, 0) // 4
        back = group + 4 * (4 - (index - 4 * group))
        fk[index] = jnp.where(member((block - back) * ROWS), 0.0, -BIG).astype(BF16)

    def head_rows(h):
        return pl.ds(pl.multiple_of(h * ROWS, ROWS), ROWS)

    def halves(tiles):
        return [t[:, half] for t in tiles for half in (slice(0, HDIM), slice(HDIM, 2 * HDIM))]

    def forward(slot, k0, c0, blocks):
        def body(h, carry):
            scores = [
                dot(qa[h], jnp.concatenate([kb[c0 + n], fk[k0 + n]], axis=1), 1, 1) for n in range(blocks)
            ]
            if slot is None:
                row = lax.broadcasted_iota(jnp.int32, (ROWS, ROWS), 0)
                column = lax.broadcasted_iota(jnp.int32, (ROWS, ROWS), 1)
                scores = [jnp.where(column <= row, scores[0], -BIG)]
            top = functools.reduce(jnp.maximum, halves(scores))
            top = jnp.max(top, axis=1, keepdims=True)
            if slot is None:
                peak = jnp.broadcast_to(top, (ROWS, HDIM))
                mb[0, h] = peak
            else:
                before = mb[slot - 1, h]
                peak = jnp.maximum(before, top)
                mb[slot, h] = peak
            peak2 = jnp.concatenate([peak, peak], axis=1) * LOG2_SCALE
            weights = [jnp.exp2(score * LOG2_SCALE - peak2) for score in scores]
            part = functools.reduce(jnp.add, halves(weights))
            for n in range(blocks):
                eb[k0 + n, head_rows(h), :] = weights[n].astype(BF16)
            if slot is None:
                tot[h] = part
            else:
                tot[h] = tot[h] * jnp.exp2((before - peak) * LOG2_SCALE) + part
            return carry

        lax.fori_loop(0, HEADS, body, 0, unroll=FWD_UNROLL)

    forward(None, 4, y * 5 + 4, 1)

    if COMM:
        for j in (1, 3, 2):
            k_y(j).wait_recv()
        for j in (1, 3, 2):
            column = lax.rem(y - j + 4, 4)
            for i in (1, 3, 2):
                k_x(i, column).start()

            @pl.when(j > y)
            def _():
                k_x(4, column).start()
        for i in (1, 3, 2, 4):
            v_x(i).wait_recv()
        for j in (1, 3, 2):
            @pl.when(y + j >= 4)
            def _():
                v_y(j, 4).start()
            for r in (3, 2, 1):
                v_y(j, r).start()
        for i in (1, 3, 2, 4):
            k_x(i, y).wait_recv()

    forward(1, 0, y * 5, 4)

    for h in range(HEADS):
        qt[:, pl.ds(h * ROWS, ROWS)] = q_ref[:, pl.ds(h * HDIM, HDIM)].T

    @pl.loop(0, 3)
    def _(step):
        j = 1 + lax.rem(2 * step, 3)
        column = lax.rem(y - j + 4, 4)
        if COMM:
            for i in (1, 2, 3):
                k_x(i, column).wait_recv()

            @pl.when(j > y)
            def _():
                k_x(4, column).wait_recv()
        forward(step + 2, 4 * j + 1, column * 5 + jnp.where(j > y, 0, 1), 4)

    for h in range(HEADS):
        norm = jnp.broadcast_to(jnp.sum(tot[h], axis=1, keepdims=True), (ROWS, HDIM))
        top = mb[4, h] * LOG2_SCALE + jnp.log2(norm)
        grad = gh[h].astype(F32)
        for slot in range(5):
            factor = jnp.exp2(mb[slot, h] * LOG2_SCALE - top)
            mb[slot, h] = factor
            scaled = (grad * factor).astype(BF16)
            gs[slot, h] = scaled
            gt[slot, :, pl.ds(h * ROWS, ROWS)] = scaled.T

    def slot_of(j):
        return jnp.where(j == 0, 1, 2 + lax.rem(2 * (j - 1), 3))

    def gk_y(j, r):
        return remote(pk.at[4 * j + r], rk.at[j - 1, r - 1], bky, (j - 1, r - 1), along_y(-j))

    def gv_x(i, c):
        back = (x < i).astype(jnp.int32)
        return remote(pv.at[c * 5 + 4 - i], rv.at[i - 1, c], bvx, (i - 1, c), along_x(-i, -back))

    def gk_x(i):
        back = (x < i).astype(jnp.int32)
        return remote(sk.at[i - 1], rk2.at[i - 1], bkx, (i - 1,), along_x(-i, -back))

    def gv_y(j):
        return remote(sv.at[j - 1], rv2.at[j - 1], bvy, (j - 1,), along_y(-j))

    @pl.loop(0, 12)
    def _(n):
        column = n // 3
        row = 1 + lax.rem(lax.rem(n, 3) + 1, 3)
        j = lax.rem(y - column + 4, 4)
        wrap = (j > y).astype(jnp.int32)
        term = dot(gt[slot_of(j)], eb[4 * j + row + wrap], 1, 0)
        pv[column * 5 + row] = term.astype(BF16)
        if COMM:
            gv_x(4 - row, column).start()

    av[...] = jnp.zeros_like(av)
    av[y] = dot(gt[0], eb[4], 1, 0)

    @pl.loop(0, 4)
    def _(j):
        column = lax.rem(y - j + 4, 4)
        wrap = (j > y).astype(jnp.int32)
        late = (j > 0) & (j <= y)
        term = dot(gt[slot_of(j)], eb[4 * j + jnp.where(late, 4, wrap)], 1, 0)

        @pl.when(late)
        def _():
            av[column] = term

        @pl.when(jnp.logical_not(late))
        def _():
            pv[column * 5] = term.astype(BF16)
            if COMM:
                gv_x(4, column).start()

    if COMM:
        for j in (1, 3, 2):
            for r in (4, 3, 2, 1):
                v_y(j, r).wait_recv()

    def output(h, carry):
        rows = head_rows(h)
        heads = pl.ds(pl.multiple_of(h * HDIM, HDIM), HDIM)
        total = mb[0, h] * dot(eb[4, rows, :], vb[4], 1, 0)
        for j in range(4):
            slot = 1 if j == 0 else 2 + (2 * (j - 1)) % 3
            k0 = 4 * j + min(j, 1)
            weights = jnp.concatenate([eb[k0 + n, rows, :] for n in range(4)], axis=1)
            total = total + mb[slot, h] * dot(weights, vb[k0 : k0 + 4].reshape(4 * ROWS, HDIM), 1, 0)
        result = total.astype(BF16)
        o_ref[:, heads] = result
        fix = jnp.sum(gh[h].astype(F32) * result.astype(F32), axis=1, keepdims=True)
        for slot in range(5):
            mb[slot, h] = mb[slot, h] * fix
        return carry

    lax.fori_loop(0, HEADS, output, 0, unroll=OUT_UNROLL)

    def values_second():
        for i in (1, 3, 2):
            for c in range(4):
                gv_x(i, c).wait_recv()
        for c in range(4):
            @pl.when(c >= y)
            def _():
                gv_x(4, c).wait_recv()
        for j in (2, 1, 3, 0):
            column = lax.rem(y - j + 4, 4)
            total = av[column]
            for i in (1, 2, 3):
                total = total + rv[i - 1, column].astype(F32)
            total = total + jnp.where(column >= y, rv[3, column].astype(F32), 0.0)
            if j > 0:
                sv[j - 1] = total.astype(BF16)
                gv_y(j).start()
            else:
                av[column] = total

    def backward(k, slot):
        for h in range(HEADS):
            rows = pl.ds(h * ROWS, ROWS)
            dprob = dot(gs[slot, h], vb[k], 1, 1)
            shift = mb[slot, h]
            shift = jnp.concatenate([shift, shift], axis=1)
            eb[k, rows, :] = (eb[k, rows, :].astype(F32) * (dprob - shift)).astype(BF16)
        return dot(qt[...], eb[k], 1, 0)

    def pass_keys(n):
        r = 1 + n // 3
        j = 1 + lax.rem(lax.rem(n, 3) + 1, 3)
        pk[4 * j + r] = backward(4 * j + r, slot_of(j)).astype(BF16)
        if COMM:
            gk_y(j, r).start()

    @pl.loop(0, 12)
    def _(n):
        pass_keys(n)
        if COMM:
            @pl.when(n == VALUES_AT)
            def _():
                values_second()

    @pl.loop(0, 5)
    def _(r):
        ak[r] = backward(r, jnp.where(r == 4, 0, 1))

    def query_grad(h, carry):
        total = None
        for k in range(17):
            j = max(k - 1, 0) // 4
            at = lax.rem(y - j + 4, 4) * 5 + k - 4 * j - jnp.where(j > y, 1, 0)
            part = dot(eb[k, head_rows(h), :], kb[at], 1, 0)
            total = part if total is None else total + part
        dq_ref[:, pl.ds(pl.multiple_of(h * HDIM, HDIM), HDIM)] = (total * SCALE).astype(BF16)
        return carry

    lax.fori_loop(0, TAIL_AT, query_grad, 0)

    if COMM:
        for j in (1, 2, 3):
            for r in (1, 2, 3, 4):
                gk_y(j, r).wait_recv()
        for h in (0, 2, 1, 3, 4):
            total = ak[h]
            for j in (1, 2, 3):
                wrap = (y + j >= 4).astype(jnp.int32)
                if h in (1, 2, 3):
                    total = total + rk[j - 1, h + wrap - 1].astype(F32)
                else:
                    hit = (wrap == 1) if h == 0 else (wrap == 0)
                    total = total + jnp.where(hit, rk[j - 1, 0 if h == 0 else 3].astype(F32), 0.0)
            if h < 4:
                sk[4 - h - 1] = total.astype(BF16)
                gk_x(4 - h).start()
            else:
                ak[h] = total

    lax.fori_loop(TAIL_AT, HEADS, query_grad, 0)

    value_total, key_total = av[y], ak[4]
    if COMM:
        for j in (1, 2, 3):
            gv_y(j).wait_recv()
            value_total = value_total + rv2[j - 1].astype(F32)
        for i in (1, 2, 3, 4):
            gk_x(i).wait_recv()
            key_total = key_total + rk2[i - 1].astype(F32)
    dv_ref[...] = value_total.T.astype(BF16)
    dk_ref[...] = (key_total * SCALE).T.astype(BF16)

    if COMM:
        for i in (1, 2, 3, 4):
            v_x(i).wait_send()
            gk_x(i).wait_send()
        for i in (1, 2, 3):
            for c in range(4):
                k_x(i, c).wait_send()
                gv_x(i, c).wait_send()
        for c in range(4):
            @pl.when(c >= y)
            def _():
                k_x(4, c).wait_send()
                gv_x(4, c).wait_send()
        for j in (1, 2, 3):
            for r in (1, 2, 3, 4):
                v_y(j, r).wait_send()
                gk_y(j, r).wait_send()
            k_y(j).wait_send()
            gv_y(j).wait_send()


CHUNKS = [(n, c) for n in (0, 1) for c in range(4)] + [(2, 0), (3, 0)]


def deliver(*refs):
    given, taken, held, sems = refs[:4], refs[4:8], refs[8:12], refs[12]

    def piece(n, c):
        return pl.ds(c * (ROWS // 4), ROWS // 4) if n < 2 else pl.ds(0, ROWS)

    def fetch(at, n, c):
        return pltpu.make_async_copy(given[n].at[piece(n, c)], held[n].at[piece(n, c)], sems.at[0, at])

    def store(at, n, c):
        return pltpu.make_async_copy(held[n].at[piece(n, c)], taken[n].at[piece(n, c)], sems.at[1, at])

    for at, chunk in enumerate(CHUNKS):
        fetch(at, *chunk).start()
    for at, chunk in enumerate(CHUNKS):
        fetch(at, *chunk).wait()
        store(at, *chunk).start()
    for at, chunk in enumerate(CHUNKS):
        store(at, *chunk).wait()


def shards(queries, keys, values, grad_out, lengths):
    vmem = pl.BlockSpec(memory_space=pltpu.VMEM)
    block = (ROWS, HDIM)
    turned = (HDIM, ROWS)
    dma = pltpu.SemaphoreType.DMA
    shapes = (
        jax.ShapeDtypeStruct((ROWS, HEADS * HDIM), BF16),
        jax.ShapeDtypeStruct((ROWS, HEADS * HDIM), BF16),
        jax.ShapeDtypeStruct(block, BF16),
        jax.ShapeDtypeStruct(block, BF16),
    )
    results = pl.pallas_call(
        kernel,
        out_shape=shapes,
        in_specs=[pl.BlockSpec(memory_space=pltpu.SMEM), vmem, vmem, vmem, vmem],
        out_specs=(vmem, vmem, vmem, vmem),
        scratch_shapes=[
            pltpu.VMEM((20,) + block, BF16),
            pltpu.VMEM((17,) + block, BF16),
            pltpu.VMEM((17,) + block, BF16),
            pltpu.VMEM((HEADS, ROWS, 2 * HDIM), BF16),
            pltpu.VMEM((HDIM, HEADS * ROWS), BF16),
            pltpu.VMEM((HEADS,) + block, BF16),
            pltpu.VMEM((5, HEADS) + block, BF16),
            pltpu.VMEM((5, HDIM, HEADS * ROWS), BF16),
            pltpu.VMEM((17, HEADS * ROWS, ROWS), BF16),
            pltpu.VMEM((5, HEADS) + block, F32),
            pltpu.VMEM((HEADS,) + block, F32),
            pltpu.VMEM((17,) + turned, BF16),
            pltpu.VMEM((20,) + turned, BF16),
            pltpu.VMEM((3, 4) + turned, BF16),
            pltpu.VMEM((4, 4) + turned, BF16),
            pltpu.VMEM((4,) + turned, BF16),
            pltpu.VMEM((3,) + turned, BF16),
            pltpu.VMEM((5,) + turned, F32),
            pltpu.VMEM((4,) + turned, F32),
            pltpu.VMEM((4,) + turned, BF16),
            pltpu.VMEM((3,) + turned, BF16),
            dma((2,)),
            dma((2, 4, 4)),
            dma((2, 3)),
            dma((2, 3, 4)),
            dma((2, 4)),
            dma((2, 3, 4)),
            dma((2, 4, 4)),
            dma((2, 4)),
            dma((2, 3)),
        ],
        compiler_params=pltpu.CompilerParams(
            collective_id=0 if COMM else None, has_side_effects=COMM, vmem_limit_bytes=67043328
        ),
        name="attention",
    )(lengths, queries, keys, values, grad_out)
    away = pl.BlockSpec(memory_space=pl.ANY)
    return pl.pallas_call(
        deliver,
        out_shape=shapes,
        in_specs=[away] * 4,
        out_specs=(away,) * 4,
        scratch_shapes=[pltpu.VMEM(shape.shape, BF16) for shape in shapes] + [dma((2, len(CHUNKS)))],
        name="deliver",
    )(*results)


def solution(mesh):
    spread = P(("dp", "ctx"), None)
    return jax.shard_map(
        shards,
        mesh=mesh,
        in_specs=(spread, spread, spread, spread, P()),
        out_specs=(spread, spread, spread, spread),
        check_vma=False,
    )
```

```python
import functools
import math

import jax
import jax.numpy as jnp
from jax import lax
from jax.experimental import pallas as pl
from jax.experimental.pallas import tpu as pltpu
from jax.sharding import PartitionSpec as P

HEADS = 8
HDIM = 128
ROWS = 256
NDOCS = 32
SCALE = float(HDIM) ** -0.5
LOG2_SCALE = SCALE * math.log2(math.e)
BIG = 2.0**20
MESH = pl.DeviceIdType.MESH
F32 = jnp.float32
BF16 = jnp.bfloat16
FWD_UNROLL = 8
OUT_UNROLL = 8
VALUES_AT = 11
TAIL_AT = 2
COMM = True


def dot(a, b, ca, cb):
    return lax.dot_general(a, b, (((ca,), (cb,)), ((), ())), preferred_element_type=F32)


def kernel(
    len_ref, q_far, k_ref, v_ref, g_far, o_ref, dq_ref, dk_ref, dv_ref,
    q_ref, g_ref, kb, vb, fk, qa, qt, gh, gs, gt, eb, mb, tot,
    pk, pv, rk, rv, rk2, rv2, ak, av, sk, sv,
    loc, kx, ky, vy, vx, bky, bvx, bkx, bvy,
):
    dp, ctx = lax.axis_index("dp"), lax.axis_index("ctx")
    x, y = ctx // 4, lax.rem(ctx, 4)
    block = dp * 16 + ctx

    def along_x(i, plane=0):
        return (lax.rem(dp + plane + 8, 8), lax.rem(x + i + 4, 4) * 4 + y)

    def along_y(j, plane=0):
        return (lax.rem(dp + plane + 8, 8), x * 4 + lax.rem(y + j + 4, 4))

    def remote(src, dst, sems, index, device):
        return pltpu.make_async_remote_copy(
            src_ref=src, dst_ref=dst, send_sem=sems.at[(0,) + index], recv_sem=sems.at[(1,) + index],
            device_id=device, device_id_type=MESH,
        )

    own = [
        pltpu.make_async_copy(k_ref, kb.at[y * 5 + 4], loc.at[0]),
        pltpu.make_async_copy(v_ref, vb.at[4], loc.at[1]),
    ]
    wide = [
        pltpu.make_async_copy(q_far, q_ref, loc.at[2]),
        pltpu.make_async_copy(g_far, g_ref, loc.at[3]),
    ]
    for copy in own + wide:
        copy.start()
    if COMM:
        barrier = pltpu.get_barrier_semaphore()

        def greet(device):
            pl.semaphore_signal(barrier, inc=1, device_id=device, device_id_type=MESH)

        for i in (1, 2, 3):
            greet(along_x(i))
            greet(along_y(i))
            greet(along_x(i, jnp.where(x + i >= 4, 1, -1)))
        greet(along_y(0, 1))
        greet(along_y(0, -1))
    for copy in own:
        copy.wait()

    def wraps(at, steps):
        return (at + steps >= 4).astype(jnp.int32)

    def v_x(i):
        return remote(v_ref, vb.at[4 - i], vx, (i - 1,), along_x(i, wraps(x, i)))

    def v_y(j, r):
        return remote(vb.at[r - wraps(y, j)], vb.at[4 * j + r], vy, (j - 1, r - 1), along_y(j))

    def k_y(j):
        return remote(k_ref, kb.at[y * 5 + 4], ky, (j - 1,), along_y(j))

    def k_x(i, c):
        return remote(kb.at[c * 5 + 4], kb.at[c * 5 + 4 - i], kx, (i - 1, c), along_x(i, wraps(x, i)))

    if COMM:
        pl.semaphore_wait(barrier, 11)
        for j in (1, 3, 2):
            k_y(j).start()
        for i in (1, 3, 2, 4):
            k_x(i, y).start()
        for i in (1, 3, 2, 4):
            v_x(i).start()
        for j in (1, 3, 2):
            @pl.when(y + j < 4)
            def _():
                v_y(j, 4).start()

    lane = lax.broadcasted_iota(jnp.int32, (1, HDIM), 1)
    starts = jnp.zeros((1, HDIM), jnp.int32)
    stops = jnp.zeros((1, HDIM), jnp.int32)
    total = jnp.int32(0)
    for d in range(NDOCS):
        starts = jnp.where(lane == d, total, starts)
        total = total + len_ref[d]
        stops = jnp.where(lane == d, total, stops)
    place = lax.broadcasted_iota(jnp.int32, (ROWS, HDIM), 0)

    def member(start):
        position = place + start
        return (position >= starts) & (position < stops)

    for copy in wide:
        copy.wait()
    query_member = jnp.where(member(block * ROWS), 1.0, 0.0).astype(BF16)
    for h in range(HEADS):
        heads = pl.ds(h * HDIM, HDIM)
        qa[h, :, :HDIM] = q_ref[:, heads]
        qa[h, :, HDIM:] = query_member
        gh[h] = g_ref[:, heads]

    @pl.loop(0, 17)
    def _(index):
        group = jnp.maximum(index - 1, 0) // 4
        back = group + 4 * (4 - (index - 4 * group))
        fk[index] = jnp.where(member((block - back) * ROWS), 0.0, -BIG).astype(BF16)

    def head_rows(h):
        return pl.ds(pl.multiple_of(h * ROWS, ROWS), ROWS)

    def halves(tiles):
        return [t[:, half] for t in tiles for half in (slice(0, HDIM), slice(HDIM, 2 * HDIM))]

    def forward(slot, k0, c0, blocks):
        def body(h, carry):
            scores = [
                dot(qa[h], jnp.concatenate([kb[c0 + n], fk[k0 + n]], axis=1), 1, 1) for n in range(blocks)
            ]
            if slot is None:
                row = lax.broadcasted_iota(jnp.int32, (ROWS, ROWS), 0)
                column = lax.broadcasted_iota(jnp.int32, (ROWS, ROWS), 1)
                scores = [jnp.where(column <= row, scores[0], -BIG)]
            top = functools.reduce(jnp.maximum, halves(scores))
            top = jnp.max(top, axis=1, keepdims=True)
            if slot is None:
                peak = jnp.broadcast_to(top, (ROWS, HDIM))
                mb[0, h] = peak
            else:
                before = mb[slot - 1, h]
                peak = jnp.maximum(before, top)
                mb[slot, h] = peak
            peak2 = jnp.concatenate([peak, peak], axis=1) * LOG2_SCALE
            weights = [jnp.exp2(score * LOG2_SCALE - peak2) for score in scores]
            part = functools.reduce(jnp.add, halves(weights))
            for n in range(blocks):
                eb[k0 + n, head_rows(h), :] = weights[n].astype(BF16)
            if slot is None:
                tot[h] = part
            else:
                tot[h] = tot[h] * jnp.exp2((before - peak) * LOG2_SCALE) + part
            return carry

        lax.fori_loop(0, HEADS, body, 0, unroll=FWD_UNROLL)

    if COMM:
        for j in (1, 3, 2):
            k_y(j).wait_recv()
            column = lax.rem(y - j + 4, 4)
            for i in (1, 3, 2):
                k_x(i, column).start()

            @pl.when(j > y)
            def _():
                k_x(4, column).start()

    forward(None, 4, y * 5 + 4, 1)

    if COMM:
        for i in (1, 3, 2, 4):
            v_x(i).wait_recv()
        for j in (1, 3, 2):
            @pl.when(y + j >= 4)
            def _():
                v_y(j, 4).start()
            for r in (3, 2, 1):
                v_y(j, r).start()
        for i in (1, 3, 2, 4):
            k_x(i, y).wait_recv()

    forward(1, 0, y * 5, 4)

    for h in range(HEADS):
        qt[:, pl.ds(h * ROWS, ROWS)] = q_ref[:, pl.ds(h * HDIM, HDIM)].T

    @pl.loop(0, 3)
    def _(step):
        j = 1 + lax.rem(2 * step, 3)
        column = lax.rem(y - j + 4, 4)
        if COMM:
            for i in (1, 2, 3):
                k_x(i, column).wait_recv()

            @pl.when(j > y)
            def _():
                k_x(4, column).wait_recv()
        forward(step + 2, 4 * j + 1, column * 5 + jnp.where(j > y, 0, 1), 4)

    for h in range(HEADS):
        norm = jnp.broadcast_to(jnp.sum(tot[h], axis=1, keepdims=True), (ROWS, HDIM))
        top = mb[4, h] * LOG2_SCALE + jnp.log2(norm)
        grad = gh[h].astype(F32)
        for slot in range(5):
            factor = jnp.exp2(mb[slot, h] * LOG2_SCALE - top)
            mb[slot, h] = factor
            scaled = (grad * factor).astype(BF16)
            gs[slot, h] = scaled
            gt[slot, :, pl.ds(h * ROWS, ROWS)] = scaled.T

    def slot_of(j):
        return jnp.where(j == 0, 1, 2 + lax.rem(2 * (j - 1), 3))

    def gk_y(j, r):
        return remote(pk.at[4 * j + r], rk.at[j - 1, r - 1], bky, (j - 1, r - 1), along_y(-j))

    def gv_x(i, c):
        back = (x < i).astype(jnp.int32)
        return remote(pv.at[c * 5 + 4 - i], rv.at[i - 1, c], bvx, (i - 1, c), along_x(-i, -back))

    def gk_x(i):
        back = (x < i).astype(jnp.int32)
        return remote(sk.at[i - 1], rk2.at[i - 1], bkx, (i - 1,), along_x(-i, -back))

    def gv_y(j):
        return remote(sv.at[j - 1], rv2.at[j - 1], bvy, (j - 1,), along_y(-j))

    @pl.loop(0, 12)
    def _(n):
        column = n // 3
        row = 1 + lax.rem(lax.rem(n, 3) + 1, 3)
        j = lax.rem(y - column + 4, 4)
        wrap = (j > y).astype(jnp.int32)
        term = dot(gt[slot_of(j)], eb[4 * j + row + wrap], 1, 0)
        pv[column * 5 + row] = term.astype(BF16)
        if COMM:
            gv_x(4 - row, column).start()

    av[...] = jnp.zeros_like(av)
    av[y] = dot(gt[0], eb[4], 1, 0)

    @pl.loop(0, 4)
    def _(j):
        column = lax.rem(y - j + 4, 4)
        wrap = (j > y).astype(jnp.int32)
        late = (j > 0) & (j <= y)
        term = dot(gt[slot_of(j)], eb[4 * j + jnp.where(late, 4, wrap)], 1, 0)

        @pl.when(late)
        def _():
            av[column] = term

        @pl.when(jnp.logical_not(late))
        def _():
            pv[column * 5] = term.astype(BF16)
            if COMM:
                gv_x(4, column).start()

    if COMM:
        for j in (1, 3, 2):
            for r in (4, 3, 2, 1):
                v_y(j, r).wait_recv()

    def output(h, carry):
        rows = head_rows(h)
        heads = pl.ds(pl.multiple_of(h * HDIM, HDIM), HDIM)
        total = mb[0, h] * dot(eb[4, rows, :], vb[4], 1, 0)
        for j in range(4):
            slot = 1 if j == 0 else 2 + (2 * (j - 1)) % 3
            k0 = 4 * j + min(j, 1)
            weights = jnp.concatenate([eb[k0 + n, rows, :] for n in range(4)], axis=1)
            total = total + mb[slot, h] * dot(weights, vb[k0 : k0 + 4].reshape(4 * ROWS, HDIM), 1, 0)
        result = total.astype(BF16)
        o_ref[:, heads] = result
        fix = jnp.sum(gh[h].astype(F32) * result.astype(F32), axis=1, keepdims=True)
        for slot in range(5):
            mb[slot, h] = mb[slot, h] * fix
        return carry

    lax.fori_loop(0, HEADS, output, 0, unroll=OUT_UNROLL)

    def values_second():
        for i in (1, 3, 2):
            for c in range(4):
                gv_x(i, c).wait_recv()
        for c in range(4):
            @pl.when(c >= y)
            def _():
                gv_x(4, c).wait_recv()
        for j in (2, 1, 3, 0):
            column = lax.rem(y - j + 4, 4)
            total = av[column]
            for i in (1, 2, 3):
                total = total + rv[i - 1, column].astype(F32)
            total = total + jnp.where(column >= y, rv[3, column].astype(F32), 0.0)
            if j > 0:
                sv[j - 1] = total.astype(BF16)
                gv_y(j).start()
            else:
                av[column] = total

    def backward(k, slot):
        for h in range(HEADS):
            rows = pl.ds(h * ROWS, ROWS)
            dprob = dot(gs[slot, h], vb[k], 1, 1)
            shift = mb[slot, h]
            shift = jnp.concatenate([shift, shift], axis=1)
            eb[k, rows, :] = (eb[k, rows, :].astype(F32) * (dprob - shift)).astype(BF16)
        return dot(qt[...], eb[k], 1, 0)

    def pass_keys(n):
        r = 1 + n // 3
        j = 1 + lax.rem(lax.rem(n, 3) + 1, 3)
        pk[4 * j + r] = backward(4 * j + r, slot_of(j)).astype(BF16)
        if COMM:
            gk_y(j, r).start()

    @pl.loop(0, 12)
    def _(n):
        pass_keys(n)
        if COMM:
            @pl.when(n == VALUES_AT)
            def _():
                values_second()

    @pl.loop(0, 5)
    def _(r):
        ak[r] = backward(r, jnp.where(r == 4, 0, 1))

    def query_grad(h, carry):
        total = None
        for k in range(17):
            j = max(k - 1, 0) // 4
            at = lax.rem(y - j + 4, 4) * 5 + k - 4 * j - jnp.where(j > y, 1, 0)
            part = dot(eb[k, head_rows(h), :], kb[at], 1, 0)
            total = part if total is None else total + part
        dq_ref[:, pl.ds(pl.multiple_of(h * HDIM, HDIM), HDIM)] = (total * SCALE).astype(BF16)
        return carry

    lax.fori_loop(0, TAIL_AT, query_grad, 0)

    if COMM:
        for j in (1, 2, 3):
            for r in (1, 2, 3, 4):
                gk_y(j, r).wait_recv()
        for h in (0, 2, 1, 3, 4):
            total = ak[h]
            for j in (1, 2, 3):
                wrap = (y + j >= 4).astype(jnp.int32)
                if h in (1, 2, 3):
                    total = total + rk[j - 1, h + wrap - 1].astype(F32)
                else:
                    hit = (wrap == 1) if h == 0 else (wrap == 0)
                    total = total + jnp.where(hit, rk[j - 1, 0 if h == 0 else 3].astype(F32), 0.0)
            if h < 4:
                sk[4 - h - 1] = total.astype(BF16)
                gk_x(4 - h).start()
            else:
                ak[h] = total

    lax.fori_loop(TAIL_AT, HEADS, query_grad, 0)

    value_total, key_total = av[y], ak[4]
    if COMM:
        for j in (1, 2, 3):
            gv_y(j).wait_recv()
            value_total = value_total + rv2[j - 1].astype(F32)
        for i in (1, 2, 3, 4):
            gk_x(i).wait_recv()
            key_total = key_total + rk2[i - 1].astype(F32)
    dv_ref[...] = value_total.T.astype(BF16)
    dk_ref[...] = (key_total * SCALE).T.astype(BF16)

    if COMM:
        for i in (1, 2, 3, 4):
            v_x(i).wait_send()
            gk_x(i).wait_send()
        for i in (1, 2, 3):
            for c in range(4):
                k_x(i, c).wait_send()
                gv_x(i, c).wait_send()
        for c in range(4):
            @pl.when(c >= y)
            def _():
                k_x(4, c).wait_send()
                gv_x(4, c).wait_send()
        for j in (1, 2, 3):
            for r in (1, 2, 3, 4):
                v_y(j, r).wait_send()
                gk_y(j, r).wait_send()
            k_y(j).wait_send()
            gv_y(j).wait_send()


CHUNKS = [(n, c) for n in (0, 1) for c in range(4)] + [(2, 0), (3, 0)]


def deliver(*refs):
    given, taken, held, sems = refs[:4], refs[4:8], refs[8:12], refs[12]

    def piece(n, c):
        return pl.ds(c * (ROWS // 4), ROWS // 4) if n < 2 else pl.ds(0, ROWS)

    def fetch(at, n, c):
        return pltpu.make_async_copy(given[n].at[piece(n, c)], held[n].at[piece(n, c)], sems.at[0, at])

    def store(at, n, c):
        return pltpu.make_async_copy(held[n].at[piece(n, c)], taken[n].at[piece(n, c)], sems.at[1, at])

    for at, chunk in enumerate(CHUNKS):
        fetch(at, *chunk).start()
    for at, chunk in enumerate(CHUNKS):
        fetch(at, *chunk).wait()
        store(at, *chunk).start()
    for at, chunk in enumerate(CHUNKS):
        store(at, *chunk).wait()


def shards(queries, keys, values, grad_out, lengths):
    vmem = pl.BlockSpec(memory_space=pltpu.VMEM)
    away = pl.BlockSpec(memory_space=pl.ANY)
    block = (ROWS, HDIM)
    turned = (HDIM, ROWS)
    dma = pltpu.SemaphoreType.DMA
    shapes = (
        jax.ShapeDtypeStruct((ROWS, HEADS * HDIM), BF16),
        jax.ShapeDtypeStruct((ROWS, HEADS * HDIM), BF16),
        jax.ShapeDtypeStruct(block, BF16),
        jax.ShapeDtypeStruct(block, BF16),
    )
    results = pl.pallas_call(
        kernel,
        out_shape=shapes,
        in_specs=[pl.BlockSpec(memory_space=pltpu.SMEM), away, vmem, vmem, away],
        out_specs=(vmem, vmem, vmem, vmem),
        scratch_shapes=[
            pltpu.VMEM((ROWS, HEADS * HDIM), BF16),
            pltpu.VMEM((ROWS, HEADS * HDIM), BF16),
            pltpu.VMEM((20,) + block, BF16),
            pltpu.VMEM((17,) + block, BF16),
            pltpu.VMEM((17,) + block, BF16),
            pltpu.VMEM((HEADS, ROWS, 2 * HDIM), BF16),
            pltpu.VMEM((HDIM, HEADS * ROWS), BF16),
            pltpu.VMEM((HEADS,) + block, BF16),
            pltpu.VMEM((5, HEADS) + block, BF16),
            pltpu.VMEM((5, HDIM, HEADS * ROWS), BF16),
            pltpu.VMEM((17, HEADS * ROWS, ROWS), BF16),
            pltpu.VMEM((5, HEADS) + block, F32),
            pltpu.VMEM((HEADS,) + block, F32),
            pltpu.VMEM((17,) + turned, BF16),
            pltpu.VMEM((20,) + turned, BF16),
            pltpu.VMEM((3, 4) + turned, BF16),
            pltpu.VMEM((4, 4) + turned, BF16),
            pltpu.VMEM((4,) + turned, BF16),
            pltpu.VMEM((3,) + turned, BF16),
            pltpu.VMEM((5,) + turned, F32),
            pltpu.VMEM((4,) + turned, F32),
            pltpu.VMEM((4,) + turned, BF16),
            pltpu.VMEM((3,) + turned, BF16),
            dma((4,)),
            dma((2, 4, 4)),
            dma((2, 3)),
            dma((2, 3, 4)),
            dma((2, 4)),
            dma((2, 3, 4)),
            dma((2, 4, 4)),
            dma((2, 4)),
            dma((2, 3)),
        ],
        compiler_params=pltpu.CompilerParams(
            collective_id=0 if COMM else None, has_side_effects=COMM, vmem_limit_bytes=67043328
        ),
        name="attention",
    )(lengths, queries, keys, values, grad_out)
    return pl.pallas_call(
        deliver,
        out_shape=shapes,
        in_specs=[away] * 4,
        out_specs=(away,) * 4,
        scratch_shapes=[pltpu.VMEM(shape.shape, BF16) for shape in shapes] + [dma((2, len(CHUNKS)))],
        name="deliver",
    )(*results)


def solution(mesh):
    spread = P(("dp", "ctx"), None)
    return jax.shard_map(
        shards,
        mesh=mesh,
        in_specs=(spread, spread, spread, spread, P()),
        out_specs=(spread, spread, spread, spread),
        check_vma=False,
    )
```
